32 devices in a mesh: section: 2 (over x), ctx: 16 (over z, y, core).
Axes of the slice: x: 2, y: 2, z: 4, core: 2. Of those that a mesh axis runs over, the one named last changes fastest.
Arguments:
- x_in: bfloat16 [512, 1536], P('ctx'), may hold values from -6 to 6
- stale_inputs: bfloat16 [2, 512, 1536], P('section', 'ctx'), may hold values from -6 to 6
- w_query: bfloat16 [2, 12, 128, 128], P('section'), may hold values from -0.5 to 0.5
- w_key: bfloat16 [2, 12, 128, 128], P('section'), may hold values from -0.5 to 0.5
- w_value: bfloat16 [2, 12, 128, 128], P('section'), may hold values from -0.5 to 0.5
- w_out: bfloat16 [2, 12, 128, 128], P('section'), may hold values from -0.5 to 0.5
- score_scale: float32 [2, 12], P('section'), may hold values from 1 to 3
- assign: int32 [512], P('ctx'), may hold values from 0 to 3, as said below
Outputs:
- section_out: bfloat16 [2, 512, 1536], P('section', 'ctx')
The draws below stay inside these ranges and needn't reach their ends.
Inputs may be any that keep to these rules, and one draw needn't show every extreme that they name: `assign`: each aligned block of 32 tokens holds the same number of tokens of every micro-batch.
All inputs are finite; a program needn't handle non-finite values.
Results may differ from the reference program's by a relative error of at most 0.013.
Values may be sent and summed in bfloat16 or wider, within the bound.
No kernel may reach another device: no remote copies, remote signals or barrier semaphores. Data moves between devices by JAX's collectives and lax.ppermute only.
A program may use at most 128 MiB of HBM per device.

```python
import math
import jax
import jax.numpy as jnp
from jax import lax

HEADS = 12
HD = 128
MB = 4
TOK_DEV = 32
HW = 1536
TOKENS = 512
N_SECTION = 2


def draw_assign(key, part):
    tile_keys = jax.random.split(key, TOKENS // TOK_DEV)
    shuffled = jax.vmap(lambda tile_key: jax.random.permutation(tile_key, TOK_DEV))(tile_keys)
    return (shuffled // (TOK_DEV // MB)).reshape(-1).astype(jnp.int32)


def steps_of(own_key, dims, pieces, smallest, largest):
    gain = 1.0
    for position, shards_of in pieces:
        heights = jax.random.uniform(jax.random.fold_in(jax.random.fold_in(own_key, 6), position), (shards_of,), jnp.float32, smallest / len(pieces), largest / len(pieces))
        gain = gain * jnp.repeat(jnp.exp(heights), dims[position] // shards_of).reshape((-1,) + (1,) * (len(dims) - 1 - position))
    return gain


def scatter_about(own_key, dims, width, bound, shards=(), kind=jnp.bfloat16):
    array = jax.random.normal(own_key, dims, jnp.float32) * width
    if len(shards) > 0:
        array = steps_of(own_key, dims, shards, -0.22, 0.18) * array
    return jnp.clip(array, min=-bound, max=bound).astype(kind)


def setup_inputs(seed: int = 0) -> dict:
    seeds = jax.random.split(jax.random.key(seed), 9)
    return {
        "x_in": scatter_about(seeds[0], (TOKENS, HW), 1.0, 6.0, ((0, 16),)),
        "stale_inputs": scatter_about(seeds[1], (N_SECTION, TOKENS, HW), 1.0, 6.0, ((0, 2), (1, 16))),
        "w_query": scatter_about(seeds[2], (N_SECTION, HEADS, HD, HD), HD ** -0.5, 0.5, ((0, 2),)),
        "w_key": scatter_about(seeds[3], (N_SECTION, HEADS, HD, HD), HD ** -0.5, 0.5, ((0, 2),)),
        "w_value": scatter_about(seeds[4], (N_SECTION, HEADS, HD, HD), HD ** -0.5, 0.5, ((0, 2),)),
        "w_out": scatter_about(seeds[5], (N_SECTION, HEADS, HD, HD), HD ** -0.5, 0.5, ((0, 2),)),
        "score_scale": jnp.clip(jnp.exp(math.log(3.0) - 1.0986123 * jax.random.uniform(seeds[6], (N_SECTION, HEADS), jnp.float32) ** steps_of(seeds[6], (N_SECTION, HEADS), ((0, 2),), -0.2, 0.2)), 1.0, 3.0),
        "assign": draw_assign(jax.random.fold_in(seeds[8], 71), 0),
    }


def normalize(values):
    floats = values.astype(jnp.float32)
    return floats * lax.rsqrt(lax.optimization_barrier(jnp.mean(floats * floats, axis=-1, keepdims=True)) + 1e-06)

def project(normed, weight):
    count = normed.shape[0]
    return jnp.einsum('nhd,hde->nhe', normed.astype(jnp.float32).reshape(count, HEADS, HD), weight.astype(jnp.float32))

def heads_of(normed, w_query, w_key, w_value, scales):
    queries = (normalize(project(normed, w_query)) * (scales[None, :, None] / math.sqrt(HD))).astype(jnp.bfloat16)
    keys = normalize(project(normed, w_key)).astype(jnp.bfloat16)
    values = project(normed, w_value).astype(jnp.bfloat16)
    return (queries, keys, values)

def layer(hidden, stale, w_query, w_key, w_value, w_out, scales, assign):
    normed = normalize(hidden).astype(jnp.bfloat16)
    queries, keys, values = heads_of(normed, w_query, w_key, w_value, scales)
    stale_normed = normalize(stale).astype(jnp.bfloat16)
    unused, stale_keys, stale_values = heads_of(stale_normed, w_query, w_key, w_value, scales)
    key_tile = jnp.arange(TOKENS, dtype=jnp.int32) // TOK_DEV
    stale_kf = stale_keys.astype(jnp.float32)
    stale_vf = stale_values.astype(jnp.float32)

    def one_tile(index):
        start = (index * TOK_DEV).astype(jnp.int32)
        tile_q = lax.dynamic_slice_in_dim(queries, start, TOK_DEV, 0).astype(jnp.float32)
        tile_k = lax.dynamic_slice_in_dim(keys, start, TOK_DEV, 0).astype(jnp.float32)
        tile_v = lax.dynamic_slice_in_dim(values, start, TOK_DEV, 0).astype(jnp.float32)
        tile_sk = lax.dynamic_slice_in_dim(stale_kf, start, TOK_DEV, 0)
        tile_sv = lax.dynamic_slice_in_dim(stale_vf, start, TOK_DEV, 0)
        tile_assign = lax.dynamic_slice_in_dim(assign, start, TOK_DEV, 0)
        far = (key_tile != index).astype(jnp.float32)
        chosen = (tile_assign[None, :] <= tile_assign[:, None]).astype(jnp.float32)
        e_far = jnp.exp(jnp.einsum('qhd,khd->hqk', tile_q, stale_kf)) * far[None, None, :]
        e_new = jnp.exp(jnp.einsum('qhd,khd->hqk', tile_q, tile_k)) * chosen[None]
        e_old = jnp.exp(jnp.einsum('qhd,khd->hqk', tile_q, tile_sk)) * (1.0 - chosen)[None]
        denom = lax.optimization_barrier(jnp.sum(e_far, -1)) + lax.optimization_barrier(jnp.sum(e_new, -1)) + lax.optimization_barrier(jnp.sum(e_old, -1))
        numer = jnp.einsum('hqk,khd->qhd', e_far.astype(jnp.bfloat16).astype(jnp.float32), stale_vf)
        numer = numer + jnp.einsum('hqk,khd->qhd', e_new.astype(jnp.bfloat16).astype(jnp.float32), tile_v)
        numer = numer + jnp.einsum('hqk,khd->qhd', e_old.astype(jnp.bfloat16).astype(jnp.float32), tile_sv)
        return (numer / jnp.transpose(denom)[:, :, None]).astype(jnp.bfloat16)
    attended = lax.map(one_tile, jnp.arange(TOKENS // TOK_DEV, dtype=jnp.int32))
    attended = attended.reshape(TOKENS, HEADS * HD)
    mixed = project(attended, w_out).reshape(TOKENS, HEADS * HD)
    return (hidden.astype(jnp.float32) + mixed).astype(jnp.bfloat16)

def reference(x_in, stale_inputs, w_query, w_key, w_value, w_out, score_scale, assign):
    hidden = x_in
    results = []
    for section in range(N_SECTION):
        hidden = layer(hidden, stale_inputs[section], w_query[section], w_key[section], w_value[section], w_out[section], score_scale[section], assign)
        results.append(hidden)
    return jnp.stack(results)
```

```python
import functools
import math

import jax
import jax.numpy as jnp
from jax import lax
from jax.experimental import pallas as pl
from jax.experimental.pallas import tpu as pltpu
from jax.sharding import PartitionSpec as P

EPS = 1e-06


def inverse_rms(floats):
    return lax.rsqrt(jnp.mean(floats * floats, axis=-1, keepdims=True) + EPS)


def normalize_rows(values):
    floats = values.astype(jnp.float32)
    return (floats * inverse_rms(floats)).astype(jnp.bfloat16)


def dot(a, b):
    return jnp.dot(a, b, preferred_element_type=jnp.float32)


def dot_t(a, b):
    return lax.dot_general(a, b, (((1,), (1,)), ((), ())), preferred_element_type=jnp.float32)


def pair_kernel(x_ref, wk_ref, wv_ref, k_ref, v_ref):
    heads, size, _ = wk_ref.shape
    normed = normalize_rows(x_ref[...])
    for head in range(heads):
        cols = slice(head * size, (head + 1) * size)
        part = normed[:, cols]
        keys = dot(part, wk_ref[head])
        k_ref[:, cols] = (keys * inverse_rms(keys)).astype(jnp.bfloat16)
        v_ref[:, cols] = dot(part, wv_ref[head]).astype(jnp.bfloat16)


def pair_call(rows_in, w_key, w_value):
    count, width = rows_in.shape
    tile = min(count, 128)
    weight = pl.BlockSpec((None,) + w_key.shape[1:], lambda i: (0, 0, 0, 0))
    block = pl.BlockSpec((tile, width), lambda i: (i, 0))
    shape = jax.ShapeDtypeStruct((count, width), jnp.bfloat16)
    return pl.pallas_call(
        pair_kernel,
        grid=(count // tile,),
        in_specs=[block, weight, weight],
        out_specs=[block, block],
        out_shape=[shape, shape],
        cost_estimate=pl.CostEstimate(
            flops=4 * count * width * w_key.shape[2],
            bytes_accessed=6 * count * width + 4 * w_key.size,
            transcendentals=0,
        ),
        name="stale_pair",
    )(rows_in, w_key, w_value)


def advance_kernel(step, chunks, flag_ref, scale_ref, acol_ref, arow_ref, h_ref, prev_ref,
                   wq_ref, wk_ref, wv_ref, wo_ref, *rest):
    k_refs = rest[:chunks]
    v_refs = rest[chunks : 2 * chunks]
    out_ref = rest[2 * chunks]
    heads, size, _ = wq_ref.shape
    tile = h_ref.shape[0]
    fresh = (arow_ref[...] <= acol_ref[...]).astype(jnp.float32)
    stale = 1.0 - fresh
    entering = h_ref[...].astype(jnp.float32)
    normed = (entering * inverse_rms(entering)).astype(jnp.bfloat16)
    mine = flag_ref[0] == step
    for head in range(heads):
        cols = slice(head * size, (head + 1) * size)
        part = normed[:, cols]
        queries = dot(part, wq_ref[head])
        factor = scale_ref[0, head] / math.sqrt(size)
        queries = (queries * inverse_rms(queries) * factor).astype(jnp.bfloat16)
        keys = dot(part, wk_ref[head])
        keys = (keys * inverse_rms(keys)).astype(jnp.bfloat16)
        values = dot(part, wv_ref[head]).astype(jnp.bfloat16)
        e_new = jnp.exp(dot_t(queries, keys)) * fresh
        denom = jnp.sum(e_new, axis=-1, keepdims=True)
        numer = dot(e_new.astype(jnp.bfloat16), values)
        for index in range(chunks):
            e_far = jnp.exp(dot_t(queries, k_refs[index][:, cols]))
            if index == 0:
                e_far = e_far * stale
            denom = denom + jnp.sum(e_far, axis=-1, keepdims=True)
            numer = numer + dot(e_far.astype(jnp.bfloat16), v_refs[index][:, cols])
        attended = (numer / denom).astype(jnp.bfloat16)
        mixed = entering[:, cols] + dot(attended, wo_ref[head])
        out_ref[:, cols] = jnp.where(mine, mixed.astype(jnp.bfloat16), prev_ref[:, cols])


def advance_call(step, flag, scales, assign, hidden, previous, weights, pairs):
    tile, width = hidden.shape
    chunks = len(pairs)
    heads, size = weights[0].shape[1:3]
    full = pl.BlockSpec(memory_space=pltpu.VMEM)
    smem = pl.BlockSpec(memory_space=pltpu.SMEM)
    tokens = sum(pair[0].shape[0] for pair in pairs) + tile
    weight = pl.BlockSpec((None,) + weights[0].shape[1:], lambda: (0, 0, 0, 0))
    return pl.pallas_call(
        functools.partial(advance_kernel, step, chunks),
        in_specs=[smem, smem] + [full] * 4 + [weight] * 4 + [full] * (2 * chunks),
        out_specs=full,
        out_shape=jax.ShapeDtypeStruct((tile, width), jnp.bfloat16),
        cost_estimate=pl.CostEstimate(
            flops=2 * tile * width * (4 * size + 2 * tokens),
            bytes_accessed=4 * tokens * width + 8 * weights[0].size,
            transcendentals=heads * tile * tokens,
        ),
        name="advance",
    )(flag, scales, assign[:, None], assign[None, :], hidden, previous, *weights,
      *[pair[0] for pair in pairs], *[pair[1] for pair in pairs])


def body(x_in, stale_inputs, w_query, w_key, w_value, w_out, score_scale, assign):
    sections = lax.axis_size("section")
    count = lax.axis_size("ctx")
    flag = lax.axis_index("section").astype(jnp.int32).reshape(1)

    held = [stale_inputs[0]]
    bit = count // 2
    while bit >= 1:
        sent = held[0] if len(held) == 1 else jnp.concatenate(held, axis=0)
        held.append(lax.ppermute(sent, "ctx", [(i, i ^ bit) for i in range(count)]))
        bit //= 2
    pairs = [pair_call(rows, w_key, w_value) for rows in held]

    weights = (w_query, w_key, w_value, w_out)
    out = x_in
    entering = x_in
    for step in range(sections):
        out = advance_call(step, flag, score_scale, assign, entering, out, weights, pairs)
        if step + 1 < sections:
            entering = lax.ppermute(out, "section", [(i, (i + 1) % sections) for i in range(sections)])
    return out[None]


def solution(mesh):
    return jax.shard_map(
        body,
        mesh=mesh,
        in_specs=(
            P("ctx", None),
            P("section", "ctx", None),
            P("section", None, None, None),
            P("section", None, None, None),
            P("section", None, None, None),
            P("section", None, None, None),
            P("section", None),
            P("ctx"),
        ),
        out_specs=P("section", "ctx", None),
        check_vma=False,
    )
```

```python
import functools
import math

import jax
import jax.numpy as jnp
from jax import lax
from jax.experimental import pallas as pl
from jax.experimental.pallas import tpu as pltpu
from jax.sharding import PartitionSpec as P

EPS = 1e-06


def inverse_rms(floats):
    return lax.rsqrt(jnp.mean(floats * floats, axis=-1, keepdims=True) + EPS)


def normalize_rows(values):
    floats = values.astype(jnp.float32)
    return (floats * inverse_rms(floats)).astype(jnp.bfloat16)


def dot(a, b):
    return jnp.dot(a, b, preferred_element_type=jnp.float32)


def dot_t(a, b):
    return lax.dot_general(a, b, (((1,), (1,)), ((), ())), preferred_element_type=jnp.float32)


def grant(*sizes):
    return min(sum(sizes) + (4 << 20), 60 << 20)


def pair_kernel(x_ref, wk_ref, wv_ref, k_ref, v_ref):
    heads, size, _ = wk_ref.shape
    normed = normalize_rows(x_ref[...])
    for head in range(heads):
        cols = slice(head * size, (head + 1) * size)
        part = normed[:, cols]
        keys = dot(part, wk_ref[head])
        k_ref[:, cols] = (keys * inverse_rms(keys)).astype(jnp.bfloat16)
        v_ref[:, cols] = dot(part, wv_ref[head]).astype(jnp.bfloat16)


def pair_call(rows_in, w_key, w_value):
    count, width = rows_in.shape
    tile = min(count, 128)
    weight = pl.BlockSpec((None,) + w_key.shape[1:], lambda i: (0, 0, 0, 0))
    block = pl.BlockSpec((tile, width), lambda i: (i, 0))
    shape = jax.ShapeDtypeStruct((count, width), jnp.bfloat16)
    return pl.pallas_call(
        pair_kernel,
        grid=(count // tile,),
        in_specs=[block, weight, weight],
        out_specs=[block, block],
        out_shape=[shape, shape],
        cost_estimate=pl.CostEstimate(
            flops=4 * count * width * w_key.shape[2],
            bytes_accessed=6 * count * width + 4 * w_key.size,
            transcendentals=0,
        ),
        compiler_params=pltpu.CompilerParams(
            vmem_limit_bytes=grant(16 * tile * width, 8 * w_key.size)
        ),
        name="stale_pair",
    )(rows_in, w_key, w_value)


def advance_kernel(step, chunks, flag_ref, scale_ref, acol_ref, arow_ref, h_ref, prev_ref,
                   wq_ref, wk_ref, wv_ref, wo_ref, *rest):
    k_refs = rest[:chunks]
    v_refs = rest[chunks : 2 * chunks]
    out_ref = rest[2 * chunks]
    heads, size, _ = wq_ref.shape
    tile = h_ref.shape[0]
    fresh = (arow_ref[...] <= acol_ref[...]).astype(jnp.float32)
    stale = 1.0 - fresh
    entering = h_ref[...].astype(jnp.float32)
    normed = (entering * inverse_rms(entering)).astype(jnp.bfloat16)
    mine = flag_ref[0] == step
    for head in range(heads):
        cols = slice(head * size, (head + 1) * size)
        part = normed[:, cols]
        queries = dot(part, wq_ref[head])
        factor = scale_ref[0, head] / math.sqrt(size)
        queries = (queries * inverse_rms(queries) * factor).astype(jnp.bfloat16)
        keys = dot(part, wk_ref[head])
        keys = (keys * inverse_rms(keys)).astype(jnp.bfloat16)
        values = dot(part, wv_ref[head]).astype(jnp.bfloat16)
        e_new = jnp.exp(dot_t(queries, keys)) * fresh
        denom = jnp.sum(e_new, axis=-1, keepdims=True)
        numer = dot(e_new.astype(jnp.bfloat16), values)
        for index in range(chunks):
            e_far = jnp.exp(dot_t(queries, k_refs[index][:, cols]))
            if index == 0:
                e_far = e_far * stale
            denom = denom + jnp.sum(e_far, axis=-1, keepdims=True)
            numer = numer + dot(e_far.astype(jnp.bfloat16), v_refs[index][:, cols])
        attended = (numer / denom).astype(jnp.bfloat16)
        mixed = entering[:, cols] + dot(attended, wo_ref[head])
        out_ref[:, cols] = jnp.where(mine, mixed.astype(jnp.bfloat16), prev_ref[:, cols])


def advance_call(step, flag, scales, assign, hidden, previous, weights, pairs):
    tile, width = hidden.shape
    chunks = len(pairs)
    heads, size = weights[0].shape[1:3]
    full = pl.BlockSpec(memory_space=pltpu.VMEM)
    smem = pl.BlockSpec(memory_space=pltpu.SMEM)
    tokens = sum(pair[0].shape[0] for pair in pairs) + tile
    weight = pl.BlockSpec((None,) + weights[0].shape[1:], lambda: (0, 0, 0, 0))
    return pl.pallas_call(
        functools.partial(advance_kernel, step, chunks),
        in_specs=[smem, smem] + [full] * 4 + [weight] * 4 + [full] * (2 * chunks),
        out_specs=full,
        out_shape=jax.ShapeDtypeStruct((tile, width), jnp.bfloat16),
        cost_estimate=pl.CostEstimate(
            flops=2 * tile * width * (4 * size + 2 * tokens),
            bytes_accessed=4 * tokens * width + 8 * weights[0].size,
            transcendentals=heads * tile * tokens,
        ),
        compiler_params=pltpu.CompilerParams(
            vmem_limit_bytes=grant(4 * tokens * width, 8 * weights[0].size, 12 * tile * width)
        ),
        name="advance",
    )(flag, scales, assign[:, None], assign[None, :], hidden, previous, *weights,
      *[pair[0] for pair in pairs], *[pair[1] for pair in pairs])


def body(x_in, stale_inputs, w_query, w_key, w_value, w_out, score_scale, assign):
    sections = lax.axis_size("section")
    count = lax.axis_size("ctx")
    flag = lax.axis_index("section").astype(jnp.int32).reshape(1)

    held = [stale_inputs[0]]
    bit = count // 2
    while bit >= 1:
        sent = held[0] if len(held) == 1 else jnp.concatenate(held, axis=0)
        held.append(lax.ppermute(sent, "ctx", [(i, i ^ bit) for i in range(count)]))
        bit //= 2
    pairs = [pair_call(rows, w_key, w_value) for rows in held]

    weights = (w_query, w_key, w_value, w_out)
    out = x_in
    entering = x_in
    for step in range(sections):
        out = advance_call(step, flag, score_scale, assign, entering, out, weights, pairs)
        if step + 1 < sections:
            entering = lax.ppermute(out, "section", [(i, (i + 1) % sections) for i in range(sections)])
    return out[None]


def solution(mesh):
    return jax.shard_map(
        body,
        mesh=mesh,
        in_specs=(
            P("ctx", None),
            P("section", "ctx", None),
            P("section", None, None, None),
            P("section", None, None, None),
            P("section", None, None, None),
            P("section", None, None, None),
            P("section", None),
            P("ctx"),
        ),
        out_specs=P("section", "ctx", None),
        check_vma=False,
    )
```

```python
import functools
import math

import jax
import jax.numpy as jnp
from jax import lax
from jax.experimental import pallas as pl
from jax.experimental.pallas import tpu as pltpu
from jax.sharding import PartitionSpec as P

EPS = 1e-06


def inverse_rms(floats):
    return lax.rsqrt(jnp.mean(floats * floats, axis=-1, keepdims=True) + EPS)


def normalize_rows(values):
    floats = values.astype(jnp.float32)
    return (floats * inverse_rms(floats)).astype(jnp.bfloat16)


def dot(a, b):
    return jnp.dot(a, b, preferred_element_type=jnp.float32)


def dot_t(a, b):
    return lax.dot_general(a, b, (((1,), (1,)), ((), ())), preferred_element_type=jnp.float32)


def grant(*sizes):
    return min(sum(sizes) + (4 << 20), 60 << 20)


def pair_kernel(x_ref, wk_ref, wv_ref, *rest):
    k_ref, v_ref = rest[-2:]
    heads, size, _ = wk_ref.shape
    normed = normalize_rows(x_ref[...])
    for head in range(heads):
        cols = slice(head * size, (head + 1) * size)
        part = normed[:, cols]
        keys = dot(part, wk_ref[head])
        k_ref[:, cols] = (keys * inverse_rms(keys)).astype(jnp.bfloat16)
        v_ref[:, cols] = dot(part, wv_ref[head]).astype(jnp.bfloat16)


def pair_call(rows_in, w_key, w_value, total, offset, tile, previous):
    count, width = rows_in.shape
    block_tiles = math.gcd(4, math.gcd(count // tile, offset // tile))
    rows = block_tiles * tile
    start = offset // rows
    weight = pl.BlockSpec((None,) + w_key.shape[1:], lambda i: (0, 0, 0, 0))
    shape = jax.ShapeDtypeStruct((total, width), jnp.bfloat16)
    out_block = pl.BlockSpec((rows, width), lambda i: (i + start, 0))
    return pl.pallas_call(
        pair_kernel,
        grid=(count // rows,),
        in_specs=[pl.BlockSpec((rows, width), lambda i: (i, 0)), weight, weight]
        + [pl.BlockSpec(memory_space=pl.ANY)] * len(previous),
        out_specs=[out_block, out_block],
        out_shape=[shape, shape],
        input_output_aliases={3 + i: i for i in range(len(previous))},
        cost_estimate=pl.CostEstimate(
            flops=4 * count * width * w_key.shape[2],
            bytes_accessed=6 * count * width + 4 * w_key.size,
            transcendentals=0,
        ),
        compiler_params=pltpu.CompilerParams(
            vmem_limit_bytes=grant(16 * rows * width, 8 * w_key.size)
        ),
        name="stale_pair",
    )(rows_in, w_key, w_value, *previous)


def copy_kernel(x_ref, o_ref):
    o_ref[...] = x_ref[...]


def copy_call(rows_in):
    whole = pl.BlockSpec(memory_space=pltpu.VMEM)
    return pl.pallas_call(
        copy_kernel,
        in_specs=[whole],
        out_specs=whole,
        out_shape=jax.ShapeDtypeStruct(rows_in.shape, rows_in.dtype),
        compiler_params=pltpu.CompilerParams(vmem_limit_bytes=4 << 20),
        name="stage",
    )(rows_in)


def advance_kernel(step, flag_ref, scale_ref, acol_ref, arow_ref, h_ref, prev_ref,
                   wq_ref, wk_ref, wv_ref, wo_ref, k_ref, v_ref, out_ref,
                   q_acc, k_acc, v_acc, e_far_ref, e_new_ref, den_ref, att_ref):
    heads, size, _ = wq_ref.shape
    tile = h_ref.shape[0]
    fresh = (arow_ref[...] <= acol_ref[...]).astype(jnp.float32)
    stale = 1.0 - fresh
    entering = h_ref[...].astype(jnp.float32)
    normed = (entering * inverse_rms(entering)).astype(jnp.bfloat16)
    mine = flag_ref[0] == step
    cols = [slice(head * size, (head + 1) * size) for head in range(heads)]
    for head in range(heads):
        part = normed[:, cols[head]]
        factor = scale_ref[0, head] / math.sqrt(size)
        queries = dot(part, wq_ref[head])
        q_acc[:, cols[head]] = (queries * inverse_rms(queries) * factor).astype(jnp.bfloat16)
        keys = dot(part, wk_ref[head])
        k_acc[:, cols[head]] = (keys * inverse_rms(keys)).astype(jnp.bfloat16)
        v_acc[:, cols[head]] = dot(part, wv_ref[head]).astype(jnp.bfloat16)
    for head in range(heads):
        queries = q_acc[:, cols[head]]
        e_far = jnp.exp(dot_t(queries, k_ref[:, cols[head]]))
        e_far = jnp.concatenate([e_far[:, :tile] * stale, e_far[:, tile:]], axis=1)
        e_new = jnp.exp(dot_t(queries, k_acc[:, cols[head]])) * fresh
        den_ref[head] = jnp.sum(e_far, axis=-1, keepdims=True) + jnp.sum(
            e_new, axis=-1, keepdims=True
        )
        e_far_ref[head] = e_far.astype(jnp.bfloat16)
        e_new_ref[head] = e_new.astype(jnp.bfloat16)
    for head in range(heads):
        numer = dot(e_far_ref[head], v_ref[:, cols[head]]) + dot(
            e_new_ref[head], v_acc[:, cols[head]]
        )
        att_ref[:, cols[head]] = (numer / den_ref[head]).astype(jnp.bfloat16)
    for head in range(heads):
        mixed = entering[:, cols[head]] + dot(att_ref[:, cols[head]], wo_ref[head])
        out_ref[:, cols[head]] = jnp.where(
            mine, mixed.astype(jnp.bfloat16), prev_ref[:, cols[head]]
        )


def advance_call(step, flag, scales, assign, hidden, previous, weights, stale_keys, stale_values):
    tile, width = hidden.shape
    heads, size = weights[0].shape[1:3]
    full = pl.BlockSpec(memory_space=pltpu.VMEM)
    smem = pl.BlockSpec(memory_space=pltpu.SMEM)
    total = stale_keys.shape[0]
    tokens = total + tile
    weight = pl.BlockSpec((None,) + weights[0].shape[1:], lambda: (0, 0, 0, 0))
    return pl.pallas_call(
        functools.partial(advance_kernel, step),
        in_specs=[smem, smem] + [full] * 4 + [weight] * 4 + [full] * 2,
        out_specs=full,
        out_shape=jax.ShapeDtypeStruct((tile, width), jnp.bfloat16),
        scratch_shapes=[pltpu.VMEM((tile, width), jnp.bfloat16)] * 3
        + [
            pltpu.VMEM((heads, tile, total), jnp.bfloat16),
            pltpu.VMEM((heads, tile, tile), jnp.bfloat16),
            pltpu.VMEM((heads, tile, 1), jnp.float32),
            pltpu.VMEM((tile, width), jnp.bfloat16),
        ],
        cost_estimate=pl.CostEstimate(
            flops=2 * tile * width * (4 * size + 2 * tokens),
            bytes_accessed=4 * tokens * width + 8 * weights[0].size,
            transcendentals=heads * tile * tokens,
        ),
        compiler_params=pltpu.CompilerParams(
            vmem_limit_bytes=grant(
                4 * total * width, 8 * weights[0].size, 24 * tile * width,
                2 * heads * tile * total,
            )
        ),
        name="advance",
    )(flag, scales, assign[:, None], assign[None, :], hidden, previous, *weights,
      stale_keys, stale_values)


def joined(parts):
    return parts[0] if len(parts) == 1 else jnp.concatenate(parts, axis=0)


def gather_groups(own):
    count = lax.axis_size("ctx")

    def move(array, bit):
        return lax.ppermute(array, "ctx", [(i, i ^ bit) for i in range(count)])

    staged = copy_call(own)
    levels = [[own]]
    bit = count // 2
    while bit > 1:
        grown = [list(level) for level in levels] + [[]]
        for hops, level in enumerate(levels):
            grown[hops + 1].append(move(joined(level), bit))
        levels = grown
        levels[0] = [own]
        bit //= 2
    levels[0] = [staged]
    if len(levels) > 2:
        levels = [levels[0] + levels[1]] + levels[2:]
    groups = []
    for level in levels:
        near = joined(level)
        groups.append(joined([near, move(near, 1)]) if count > 1 else near)
    return groups


def body(x_in, stale_inputs, w_query, w_key, w_value, w_out, score_scale, assign):
    sections = lax.axis_size("section")
    tile = x_in.shape[0]
    flag = lax.axis_index("section").astype(jnp.int32).reshape(1)

    groups = gather_groups(stale_inputs[0])
    total = sum(group.shape[0] for group in groups)
    pair, offset = (), 0
    for group in groups:
        pair = pair_call(group, w_key, w_value, total, offset, tile, pair)
        offset += group.shape[0]

    weights = (w_query, w_key, w_value, w_out)
    out = x_in
    entering = x_in
    for step in range(sections):
        out = advance_call(step, flag, score_scale, assign, entering, out, weights, *pair)
        if step + 1 < sections:
            entering = lax.ppermute(out, "section", [(i, (i + 1) % sections) for i in range(sections)])
    return out[None]


def solution(mesh):
    return jax.shard_map(
        body,
        mesh=mesh,
        in_specs=(
            P("ctx", None),
            P("section", "ctx", None),
            P("section", None, None, None),
            P("section", None, None, None),
            P("section", None, None, None),
            P("section", None, None, None),
            P("section", None),
            P("ctx"),
        ),
        out_specs=P("section", "ctx", None),
        check_vma=False,
    )
```
